512 devices in a mesh: dom: 32 (over y, x), grp: 16 (over z, core).
Axes of the slice: x: 4, y: 8, z: 8, core: 2. Of those that a mesh axis runs over, the one named last changes fastest.
Arguments:
- positions: float32 [3, 262144], P(None, ('dom', 'grp')), may hold values from -6 to 6
- mass: float32 [262144], P(('dom', 'grp')), may hold values from 0.05 to 0.2
- smooth: float32 [262144], P(('dom', 'grp')), may hold values from 1.5 to 3.5
- counts: int32 [1024], P(('dom', 'grp')), may hold values from 128 to 256
- tasks: int32 [2, 2048], P(None, ('dom', 'grp')), may hold values from 0 to 95, as said below
Outputs:
- density: float32 [262144], P(('dom', 'grp'))
- accel: float32 [3, 262144], P(None, ('dom', 'grp'))
The draws below stay inside these ranges and needn't reach their ends.
Inputs may be any that keep to these rules, and one draw needn't show every extreme that they name: In every slab, for each b the slab's tasks whose receiving cell lies among slab cells b * 2 to (b + 1) * 2 - 1 number at most 12, and exactly 12 for one b; a cell may receive no task.
All inputs are finite; a program needn't handle non-finite values.
Results may differ from the reference program's by a relative error of at most 0.00017.
Values sent between devices are 32-bit elements; how exact they have to be, the bound alone decides.
No kernel may reach another device: no remote copies, remote signals or barrier semaphores. Data moves between devices by JAX's collectives and lax.ppermute only.
A program may use at most 64 MiB of HBM per device.

```python
import math
import jax
import jax.numpy as jnp
from jax import lax

CELL = 256
CD = 2
PT = 4
OCAP = 12
CELLS = 1024
TASKS = 2048
PARTICLES = 262144
N_DOM = 32
N_GRP = 16


def slab_receivers(single):
    busy_key = jax.random.fold_in(single, 3)
    cell_key = jax.random.fold_in(single, 5)
    perm_key = jax.random.fold_in(single, 7)
    total = N_GRP * PT
    busy = jax.random.randint(busy_key, (), 0, N_GRP)
    ranks = jnp.arange(total, dtype=jnp.int32)
    others = jnp.maximum(ranks - OCAP, 0) % (N_GRP - 1)
    others = jnp.where(others >= busy, others + 1, others)
    blocks = jnp.where(ranks < OCAP, busy, others)
    inner = jax.random.randint(cell_key, (total,), 0, CD)
    receivers = (blocks * CD + inner).astype(jnp.int32)
    shuffle = jax.random.permutation(perm_key, total)
    return receivers[shuffle]


def draw_tasks(key, part):
    first_key = jax.random.fold_in(key, 11)
    second_key = jax.random.fold_in(key, 23)
    slab_cells = N_GRP * CD
    keys = jax.random.split(first_key, N_DOM)
    receivers = jax.vmap(slab_receivers)(keys).reshape(TASKS).astype(jnp.int32)
    sources = jax.random.randint(second_key, (TASKS,), 0, 3 * slab_cells).astype(jnp.int32)
    return jnp.stack([receivers, sources], 0)


def plant(array, own_key, low, largest):
    dims = array.shape
    place = [jax.random.randint(jax.random.fold_in(own_key, axis), (), 0, dims[axis]) for axis in range(len(dims))]
    array = array.at[tuple(place)].set(low)
    longest = dims.index(max(dims))
    place[longest] = (place[longest] + 1) % dims[longest]
    return array.at[tuple(place)].set(largest)


def level_of(stream_key, dims, pieces, smallest, high):
    level, own = 1.0, jax.random.fold_in(stream_key, 6)
    for dim, blocks in pieces:
        heights = jnp.exp(jax.random.uniform(jax.random.fold_in(own, dim), (blocks,), jnp.float32, smallest / len(pieces), high / len(pieces)))
        level = level * jnp.repeat(heights, dims[dim] // blocks).reshape([-1 if axis == dim else 1 for axis in range(len(dims))])
    return level


def normal_values(own_key, dims, scale, bound, cuts=(), held_as=jnp.bfloat16):
    array = jax.random.normal(own_key, dims, jnp.float32) * scale
    if len(cuts) > 0:
        array = level_of(own_key, dims, cuts, -0.22, 0.18) * array
    return jnp.clip(array, min=-bound, max=bound).astype(held_as)


def setup_inputs(seed: int = 0) -> dict:
    arg_keys = jax.random.split(jax.random.key(seed), 6)
    positions = normal_values(arg_keys[0], (3, PARTICLES), 1.0, 6.0, ((1, 512),), jnp.float32)
    mass = jnp.clip(jnp.exp(math.log(0.2) - 1.3862944 * jax.random.uniform(arg_keys[1], (PARTICLES,), jnp.float32) ** level_of(arg_keys[1], (PARTICLES,), ((0, 512),), -0.2, 0.2)), 0.05, 0.2)
    smooth = jnp.clip(jnp.exp(math.log(3.5) - 0.84729786 * jax.random.uniform(arg_keys[2], (PARTICLES,), jnp.float32) ** level_of(arg_keys[2], (PARTICLES,), ((0, 512),), -0.2, 0.2)), 1.5, 3.5)
    counts = plant(jax.random.randint(arg_keys[3], (CELLS,), 128, 257), jax.random.fold_in(arg_keys[3], 1), 128, 256).astype(jnp.int32)
    tasks = draw_tasks(jax.random.fold_in(arg_keys[5], 71), 0)
    return dict(positions=positions, mass=mass, smooth=smooth, counts=counts, tasks=tasks)


def tile_terms(recv, source):
    diff_x = recv[0][:, None] - source[0][None, :]
    diff_y = recv[1][:, None] - source[1][None, :]
    diff_z = recv[2][:, None] - source[2][None, :]
    radius = jnp.sqrt(diff_x * diff_x + diff_y * diff_y + diff_z * diff_z)
    length = recv[4][:, None]
    inside = jnp.maximum(1.0 - radius / length, 0.0)
    return (diff_x, diff_y, diff_z, radius, length, inside)

def density_tile(recv, source):
    diff_x, diff_y, diff_z, radius, length, inside = tile_terms(recv, source)
    weight = inside ** 4 * (1.0 + 4.0 * radius / length) * (21.0 / (2.0 * math.pi)) / length ** 3
    return lax.optimization_barrier(jnp.sum(weight * source[3][None, :], axis=1))

def force_tile(recv, source, rho_recv, rho_source):
    diff_x, diff_y, diff_z, radius, length, inside = tile_terms(recv, source)
    coeff = source[3][None, :] * (1.0 / rho_recv[:, None] + 1.0 / rho_source[None, :])
    coeff = coeff * inside ** 3 * (105.0 / math.pi) / length ** 5
    return jnp.stack([lax.optimization_barrier(jnp.sum(coeff * diff_x, 1)), lax.optimization_barrier(jnp.sum(coeff * diff_y, 1)), lax.optimization_barrier(jnp.sum(coeff * diff_z, 1))], 0)

def reference(positions, mass, smooth, counts, tasks):
    cells = counts.shape[0]
    live = (jnp.arange(CELL, dtype=jnp.int32)[None, :] < counts[:, None]).astype(jnp.float32)
    mass_cells = mass.reshape(cells, CELL)
    smooth_cells = smooth.reshape(cells, CELL)
    packed = jnp.concatenate([positions.reshape(3, cells, CELL), (mass_cells * live)[None], smooth_cells[None]], 0)
    slab_cells = N_GRP * CD
    order = jnp.arange(TASKS, dtype=jnp.int32)
    slab_of = order // (N_GRP * PT)
    recv_cell = (slab_of * slab_cells + tasks[0]).astype(jnp.int32)
    side = tasks[1] // slab_cells
    source_cell = ((slab_of + side - 1) % N_DOM * slab_cells + tasks[1] % slab_cells).astype(jnp.int32)

    def dens(pair):
        return density_tile(packed[:, pair[0]], packed[:, pair[1]])
    partial_value = lax.map(dens, (recv_cell, source_cell), batch_size=64)
    self_term = mass_cells * (21.0 / (2.0 * math.pi)) / smooth_cells ** 3
    rho = self_term + jax.ops.segment_sum(partial_value, recv_cell, num_segments=cells)

    def force(pair):
        return force_tile(packed[:, pair[0]], packed[:, pair[1]], rho[pair[0]], rho[pair[1]])
    force_part = lax.map(force, (recv_cell, source_cell), batch_size=64)
    accel = jax.ops.segment_sum(force_part, recv_cell, num_segments=cells)
    accel = jnp.transpose(accel * live[:, None, :], (1, 0, 2)).reshape(3, cells * CELL)
    density = (rho * live).reshape(cells * CELL)
    return (density, accel)
```

```python
import math

import jax
import jax.numpy as jnp
from jax import lax
from jax.experimental import pallas as pl
from jax.experimental.pallas import tpu as pltpu
from jax.sharding import PartitionSpec as P

CELL = 256
LANES = 128
ROWS = 24
FAR = 16
BLOCK = 3 * ROWS + 2 * FAR
NORM_W = 21.0 / (2.0 * math.pi)
NORM_F = 105.0 / math.pi
TINY = 1e-30


def pack_kernel(counts_ref, tasks_ref, pos_ref, mass_ref, smooth_ref, out_ref):
    lane = lax.broadcasted_iota(jnp.int32, (1, LANES), 1)
    for j in range(2):
        for c in range(2):
            row = 2 * j + c
            cut = pl.ds(row * LANES, LANES)
            for axis in range(3):
                out_ref[4 * axis + row : 4 * axis + row + 1, :] = pos_ref[axis : axis + 1, cut]
            live = lane + c * LANES < counts_ref[j]
            out_ref[12 + row : 13 + row, :] = jnp.where(live, mass_ref[cut].reshape(1, LANES), 0.0)
            out_ref[16 + row : 17 + row, :] = smooth_ref[cut].reshape(1, LANES)
    codes = jnp.zeros((1, LANES), jnp.float32)
    for i in range(8):
        codes = jnp.where(lane == i, tasks_ref[i // 4, i % 4].astype(jnp.float32), codes)
    out_ref[20:21, :] = codes
    out_ref[21:24, :] = jnp.zeros((3, LANES), jnp.float32)


def slab_base(slab):
    return jnp.maximum(slab * ROWS - (ROWS - FAR), 0)


def row_of(slab, cell):
    return (cell // 2) * BLOCK + slab_base(slab) + 2 * (cell % 2)


def main_kernel(
    member_of, g_ref, dens_ref, acc_ref, tvm, tsm, sem, head, nxt, done,
    xb, yb, zb, hb, ib, fx, fy, fz, wrow, irow,
):
    for s in range(3):
        for m in range(16):
            r = m * BLOCK + s * ROWS + FAR + 20
            tvm[s * 16 + m : s * 16 + m + 1, :] = g_ref[r : r + 1, :].astype(jnp.int32)
    copy = pltpu.make_async_copy(tvm, tsm, sem)
    copy.start()
    copy.wait()

    def clear(i, _):
        head[i] = -1
        done[i] = 0
        return 0

    lax.fori_loop(0, 96, clear, 0)

    def link(u, _):
        s = u // 16
        for i in range(4):
            cell = s * 32 + tsm[u, i]
            nxt[u * 4 + i] = head[cell]
            head[cell] = u * 4 + i
        return 0

    lax.fori_loop(0, 48, link, 0)

    def task_source(t):
        u = t // 4
        k = tsm[u, 4 + t % 4]
        slab = u // 16 + k // 32
        return slab, k % 32

    def columns(rows, refs):
        for c in range(2):
            block = jnp.concatenate([r[c] for r in rows] + [rows[0][c]] * (8 - len(rows)), 0)
            turned = jnp.transpose(block)
            for q in range(len(rows)):
                refs[q][c * LANES : (c + 1) * LANES, :] = jnp.broadcast_to(
                    turned[:, q : q + 1], (LANES, LANES)
                )

    def rows_at(row0, q):
        return [g_ref[pl.ds(row0 + 4 * q + c, 1), :] for c in range(2)]

    def lane_sums(ref):
        out = lax.dot_general(
            jnp.ones((8, LANES), jnp.float32), ref[...], (((1,), (1,)), ((), ())),
            precision=lax.Precision.HIGHEST, preferred_element_type=jnp.float32,
        )
        return [out[0:1, 0:LANES], out[0:1, LANES : 2 * LANES]]

    def spread(row):
        return jnp.broadcast_to(g_ref[pl.ds(row, 1), :], (8, LANES))

    def cell_density(cell):
        slab = cell // 32 + 1
        row0 = row_of(slab, cell % 32)
        h = rows_at(row0, 4)
        columns([rows_at(row0, 0), rows_at(row0, 1), rows_at(row0, 2), [1.0 / v for v in h]], [xb, yb, zb, hb])
        fx[...] = jnp.zeros((CELL, LANES), jnp.float32)

        def tile(t):
            sslab, scell = task_source(t)
            srow = row_of(sslab, scell)
            src = [[spread(srow + 4 * q + c) for q in range(4)] for c in range(2)]
            for i in range(CELL // 8):
                cut = slice(8 * i, 8 * i + 8)
                x, y, z, ih = xb[cut, :], yb[cut, :], zb[cut, :], hb[cut, :]
                total = fx[cut, :]
                for c in range(2):
                    dx, dy, dz = x - src[c][0], y - src[c][1], z - src[c][2]
                    r2 = dx * dx + dy * dy + dz * dz
                    r = r2 * lax.rsqrt(jnp.maximum(r2, TINY))
                    t1 = jnp.maximum(1.0 - r * ih, 0.0)
                    t2 = t1 * t1
                    total = total + (t2 * t2) * (5.0 - 4.0 * t1) * src[c][3]
                fx[cut, :] = total
            return nxt[t]

        lax.while_loop(lambda t: t >= 0, tile, head[cell])
        sums = lane_sums(fx)
        mass = rows_at(row0, 3)
        return [(sums[c] + mass[c]) * (NORM_W / (h[c] * h[c] * h[c])) for c in range(2)], mass

    def weigh(cell):
        rho, mass = cell_density(cell)
        for c in range(2):
            wrow[pl.ds(2 * cell + c, 1), :] = jnp.where(mass[c] > 0.0, mass[c] / rho[c], 0.0)
        done[cell] = 1
        return rho, mass

    member = member_of()
    for j in range(2):
        rho, mass = weigh(32 + 2 * member + j)
        for c in range(2):
            r = 2 * j + c
            dens_ref[pl.ds(r * LANES, LANES)] = jnp.where(mass[c] > 0.0, rho[c], 0.0).reshape(LANES)
            irow[r : r + 1, :] = jnp.where(mass[c] > 0.0, 1.0 / rho[c], 0.0)

    for j in range(2):

        def need(t):
            sslab, scell = task_source(t)
            cell = (sslab - 1) * 32 + scell

            @pl.when(done[cell] == 0)
            def _():
                weigh(cell)

            return nxt[t]

        lax.while_loop(lambda t: t >= 0, need, head[32 + 2 * member + j])

    for j in range(2):
        cell = 32 + 2 * member + j
        row0 = row_of(2, 2 * member + j)
        h = rows_at(row0, 4)
        mass = rows_at(row0, 3)
        inv = [irow[2 * j + c : 2 * j + c + 1, :] for c in range(2)]
        columns(
            [rows_at(row0, 0), rows_at(row0, 1), rows_at(row0, 2), [1.0 / v for v in h], inv],
            [xb, yb, zb, hb, ib],
        )
        for f in (fx, fy, fz):
            f[...] = jnp.zeros((CELL, LANES), jnp.float32)

        def tile(t):
            sslab, scell = task_source(t)
            srow = row_of(sslab, scell)
            wcell = (sslab - 1) * 32 + scell
            src = [[spread(srow + 4 * q + c) for q in range(4)] for c in range(2)]
            wts = [jnp.broadcast_to(wrow[pl.ds(2 * wcell + c, 1), :], (8, LANES)) for c in range(2)]
            for i in range(CELL // 8):
                cut = slice(8 * i, 8 * i + 8)
                x, y, z, ih, ir = xb[cut, :], yb[cut, :], zb[cut, :], hb[cut, :], ib[cut, :]
                ax, ay, az = fx[cut, :], fy[cut, :], fz[cut, :]
                for c in range(2):
                    dx, dy, dz = x - src[c][0], y - src[c][1], z - src[c][2]
                    r2 = dx * dx + dy * dy + dz * dz
                    r = r2 * lax.rsqrt(jnp.maximum(r2, TINY))
                    t1 = jnp.maximum(1.0 - r * ih, 0.0)
                    coeff = (src[c][3] * ir + wts[c]) * (t1 * t1 * t1)
                    ax, ay, az = ax + coeff * dx, ay + coeff * dy, az + coeff * dz
                fx[cut, :] = ax
                fy[cut, :] = ay
                fz[cut, :] = az
            return nxt[t]

        lax.while_loop(lambda t: t >= 0, tile, head[cell])
        for axis, f in enumerate((fx, fy, fz)):
            sums = lane_sums(f)
            for c in range(2):
                h2 = h[c] * h[c]
                scale = NORM_F / (h2 * h2 * h[c])
                acc_ref[axis : axis + 1, pl.ds((2 * j + c) * LANES, LANES)] = jnp.where(
                    mass[c] > 0.0, sums[c] * scale, 0.0
                )


def main_call(pool, member_of, interpret=False):
    big = pltpu.VMEM((CELL, LANES), jnp.float32)
    return pl.pallas_call(
        lambda *refs: main_kernel(member_of, *refs),
        out_shape=(jax.ShapeDtypeStruct((512,), jnp.float32), jax.ShapeDtypeStruct((3, 512), jnp.float32)),
        in_specs=[pl.BlockSpec(memory_space=pltpu.VMEM)],
        out_specs=(pl.BlockSpec(memory_space=pltpu.VMEM), pl.BlockSpec(memory_space=pltpu.VMEM)),
        scratch_shapes=[
            pltpu.VMEM((48, LANES), jnp.int32),
            pltpu.SMEM((48, LANES), jnp.int32),
            pltpu.SemaphoreType.DMA,
            pltpu.SMEM((96,), jnp.int32),
            pltpu.SMEM((192,), jnp.int32),
            pltpu.SMEM((96,), jnp.int32),
        ]
        + [big] * 8
        + [pltpu.VMEM((192, LANES), jnp.float32), pltpu.VMEM((8, LANES), jnp.float32)],
        interpret=interpret,
        name="sph",
    )(pool)


def pack_call(positions, mass, smooth, counts, tasks, interpret=False):
    smem = pl.BlockSpec(memory_space=pltpu.SMEM)
    vmem = pl.BlockSpec(memory_space=pltpu.VMEM)
    return pl.pallas_call(
        pack_kernel,
        out_shape=jax.ShapeDtypeStruct((ROWS, LANES), jnp.float32),
        in_specs=[smem, smem, vmem, vmem, vmem],
        out_specs=vmem,
        interpret=interpret,
        name="pack",
    )(counts, tasks, positions, mass, smooth)


def shifted(block, step):
    count = lax.axis_size("dom")
    return lax.ppermute(block, "dom", [(i, (i + step) % count) for i in range(count)])


def local(positions, mass, smooth, counts, tasks):
    block = pack_call(positions, mass, smooth, counts, tasks)
    low, high = shifted(block, 1), shifted(block, -1)
    low2, high2 = shifted(block, 2), shifted(block, -2)
    wide = jnp.concatenate([low2[:FAR], low, block, high, high2[:FAR]], 0)
    pool = lax.all_gather(wide, "grp", axis=0, tiled=True)
    return main_call(pool, lambda: lax.axis_index("grp"))


def solution(mesh):
    in_specs = (
        P(None, ("dom", "grp")),
        P(("dom", "grp")),
        P(("dom", "grp")),
        P(("dom", "grp")),
        P(None, ("dom", "grp")),
    )
    out_specs = (P(("dom", "grp")), P(None, ("dom", "grp")))
    return jax.shard_map(local, mesh=mesh, in_specs=in_specs, out_specs=out_specs, check_vma=False)
```

```python
import math

import jax
import jax.numpy as jnp
from jax import lax
from jax.experimental import pallas as pl
from jax.experimental.pallas import tpu as pltpu
from jax.sharding import PartitionSpec as P

CELL = 256
LANES = 128
ROWS = 24
FAR = 16
BLOCK = 3 * ROWS + 2 * FAR
NORM_W = 21.0 / (2.0 * math.pi)
NORM_F = 105.0 / math.pi
TINY = 1e-30


def pack_kernel(member_of, counts_ref, tasks_ref, pos_ref, mass_ref, smooth_ref, out_ref):
    lane = lax.broadcasted_iota(jnp.int32, (1, LANES), 1)
    for j in range(2):
        for c in range(2):
            row = 2 * j + c
            cut = pl.ds(row * LANES, LANES)
            for axis in range(3):
                out_ref[4 * axis + row : 4 * axis + row + 1, :] = pos_ref[axis : axis + 1, cut]
            live = lane + c * LANES < counts_ref[j]
            out_ref[12 + row : 13 + row, :] = jnp.where(live, mass_ref[cut].reshape(1, LANES), 0.0)
            out_ref[16 + row : 17 + row, :] = smooth_ref[cut].reshape(1, LANES)
    codes = jnp.zeros((1, LANES), jnp.float32)
    place = lane - 4 * member_of()
    for i in range(4):
        codes = jnp.where(place == i, tasks_ref[0, i].astype(jnp.float32), codes)
        codes = jnp.where(place == 64 + i, tasks_ref[1, i].astype(jnp.float32), codes)
    out_ref[20:21, :] = codes
    out_ref[21:24, :] = jnp.zeros((3, LANES), jnp.float32)


def slab_base(slab):
    near = slab * ROWS + (2 * FAR - ROWS)
    return jnp.where(slab == 0, 0, jnp.where(slab == 4, FAR, near))


def row_of(slab, cell):
    return (cell // 2) * BLOCK + slab_base(slab) + 2 * (cell % 2)


def split3(v):
    a = v.astype(jnp.bfloat16).astype(jnp.float32)
    b = (v - a).astype(jnp.bfloat16).astype(jnp.float32)
    return a, b, v - a - b


def stack16(*parts):
    return jnp.concatenate(parts, 0).astype(jnp.bfloat16)


def main_kernel(
    member_of, g_ref, dens_ref, acc_ref, tvm, tsm, sem, done, isrc, ircv, islot, ikeep, ilive,
    fsrc, fslot, fcell, fkeep, flive, l0, l1, r0, r1, m0, m1, q0, q1, rrow, orow,
):
    wide = (64, LANES)
    lane = lax.broadcasted_iota(jnp.int32, wide, 1)
    other = lax.broadcasted_iota(jnp.int32, wide, 0)
    codes = []
    for s in range(3):
        at = 2 * FAR + s * ROWS + 20
        both = jnp.concatenate([g_ref[m * BLOCK + at : m * BLOCK + at + 1, :] for m in range(16)], 0)
        codes.append(jnp.sum(both, 0, keepdims=True))
    turned = jnp.transpose(jnp.concatenate(codes + [jnp.zeros((5, LANES), jnp.float32)], 0))
    lane1 = lax.broadcasted_iota(jnp.int32, (1, LANES), 1)
    lists = []
    for s in range(3):
        mine = jnp.broadcast_to(turned[0:64, s : s + 1], wide).astype(jnp.int32)
        code = codes[s].astype(jnp.int32)
        theirs = jnp.broadcast_to(code, wide)
        later = jnp.max(jnp.where((mine == theirs) & (other < lane), other, -1), 0, keepdims=True)
        head = jnp.max(jnp.where(mine == lane - 64, other, -1), 0, keepdims=True)
        slab = lax.shift_right_logical(code, 5) + s
        cell = code & 31
        base = jnp.where(slab == 0, 0, jnp.where(slab == 4, FAR, slab * ROWS + (2 * FAR - ROWS)))
        where = lax.shift_right_logical(cell, 1) * BLOCK + base + 2 * (cell & 1)
        lists.append(jnp.where(lane1 < 64, later, where))
        lists.append(jnp.where(lane1 < 64, (slab - 1) * 32 + cell, head))
        lists.append((slab - 1) * 32 + cell)
    tvm[...] = jnp.concatenate(lists + [jnp.zeros((7, LANES), jnp.int32)], 0)
    copy = pltpu.make_async_copy(tvm, tsm, sem)
    copy.start()

    def clear(i, _):
        for k in range(16):
            done[16 * i + k] = 0
        return 0

    lax.fori_loop(0, 6, clear, 0)
    orow[...] = jnp.zeros((48, LANES), jnp.float32)
    member = member_of()
    home = row_of(2, 2 * member)
    copy.wait()

    def list_cell(cell, n):
        s = lax.shift_right_logical(cell, 5)
        c = cell & 31
        rcv = lax.shift_right_logical(c, 1) * BLOCK + s * ROWS + 2 * FAR + 2 * (c & 1)
        slot = 2 * cell
        ahead = 3 * s

        def put(n, src, keep, live):
            isrc[n] = src
            ircv[n] = rcv
            islot[n] = slot
            ikeep[n] = keep
            ilive[n] = live

        def add(state):
            t, n = state
            put(n, tsm[ahead, 64 + t], 1.0, 1.0)
            return tsm[ahead, t], n + 1

        put(n, rcv, 0.0, 0.0)
        _, last = lax.while_loop(lambda s: s[0] >= 0, add, (tsm[ahead + 1, 64 + c], n))
        ikeep[n] = 0.0
        done[cell] = 1
        return jnp.maximum(last, n + 1)

    count = jnp.int32(0)
    total = jnp.int32(0)
    for j in range(2):
        cell = 32 + 2 * member + j
        count = list_cell(cell, count)
        start = total

        def own(state, j=j):
            t, n = state
            fsrc[n] = tsm[3, 64 + t]
            fslot[n] = tsm[5, 64 + t]
            fcell[n] = j
            fkeep[n] = 1.0
            flive[n] = 1.0
            return tsm[3, t], n + 1

        _, total = lax.while_loop(lambda s: s[0] >= 0, own, (tsm[4, 64 + 2 * member + j], total))
        fkeep[start] = 0.0

    def need(i, n):
        cell = fslot[i]
        return lax.cond(done[cell] == 0, lambda n: list_cell(cell, n), lambda n: n, n)

    count = lax.fori_loop(0, total, need, count)
    for k in range(6):
        isrc[count + k] = home
        ircv[count + k] = home
        islot[count + k] = 192
        ikeep[count + k] = 0.0
        ilive[count + k] = 0.0
        fsrc[total + k] = home
        fslot[total + k] = 32 + 2 * member
        fcell[total + k] = 2
        fkeep[total + k] = 0.0
        flive[total + k] = 0.0

    sub = lax.broadcasted_iota(jnp.int32, (8, LANES), 0)
    space = sub < 3
    pad = jnp.zeros((2, LANES), jnp.float32)

    def rows8(row):
        return jnp.concatenate([g_ref[pl.ds(row, 6, stride=4), :], pad], 0)

    def spread(v, k):
        return jnp.broadcast_to(v[k : k + 1, :], (8, LANES))

    def centre(rcv):
        return jnp.where(space, jnp.broadcast_to(rows8(rcv)[:, 0:1], (8, LANES)), 0.0)

    def square(d):
        return jnp.broadcast_to(jnp.sum(jnp.where(space, d * d, 0.0), 0, keepdims=True), (8, LANES))

    lanes8 = lax.broadcasted_iota(jnp.int32, (48, LANES), 0)
    pick_mass = jnp.where((lanes8 == 5) | (lanes8 == 13) | (lanes8 == 37), 1.0, 0.0).astype(jnp.bfloat16)
    for r_ref in (r0, r1):
        r_ref[:, 2 * LANES : 3 * LANES] = pick_mass

    def prepare(src, rcv, live, l_ref, r_ref):
        mid = centre(rcv)
        out = []
        for c in range(2):
            d = rows8(src + c) - mid
            out.append(d)
            b = jnp.where(space, d, jnp.where(sub == 3, 1.0, jnp.where(sub == 4, square(d), 0.0)))
            b = jnp.where(sub == 5, spread(d, 3) * live, b)
            b1, b2, b3 = split3(b)
            pair = stack16(b1, b2)
            left = jnp.concatenate([pair, pair, stack16(b3, b1)], 0)
            l_ref[c * LANES : (c + 1) * LANES, 0:48] = jnp.transpose(left)
            v = rows8(rcv + c)
            d = v - mid
            h = spread(v, 4)
            s = 1.0 / (h * h)
            a = jnp.where(space, -2.0 * d, jnp.where(sub == 3, square(d), jnp.where(sub == 4, 1.0, 0.0))) * s
            a1, a2, a3 = split3(a)
            r_ref[:, c * LANES : (c + 1) * LANES] = jnp.concatenate(
                [stack16(a1, a1), stack16(a2, a2), stack16(a1, a3)], 0
            )
        return out

    def multiply(l_ref, r_ref, q_ref, width):
        q_ref[:, 0:width] = jnp.dot(
            l_ref[:, 0:48], r_ref[:, 0:width], preferred_element_type=jnp.float32
        )

    def nearness(q2):
        q2 = jnp.maximum(q2, TINY)
        return jnp.maximum(1.0 - q2 * lax.rsqrt(q2), 0.0)

    def kernel_sum(n, q_ref, before):
        keep = ikeep[n]
        acc = [v * keep for v in before]
        for g in range(CELL // 8):
            cut = slice(8 * g, 8 * g + 8)
            m = q_ref[cut, 2 * LANES : 3 * LANES]
            for c in range(2):
                t = nearness(q_ref[cut, c * LANES : (c + 1) * LANES])
                t2 = t * t
                acc[c] = acc[c] + (t2 * t2) * (1.25 - t) * m
        return acc

    def row(r, q):
        return g_ref[pl.ds(r + 4 * q, 1), :]

    def finish(n, acc):
        rcv, slot = ircv[n], islot[n]
        for c in range(2):
            h = row(rcv + c, 4)
            total = 4.0 * jnp.sum(acc[c], 0, keepdims=True) + row(rcv + c, 3)
            rrow[pl.ds(slot + c, 1), :] = total * (NORM_W / (h * h * h))

    zero = jnp.zeros((8, LANES), jnp.float32)

    def ready(n, l_ref, r_ref):
        prepare(isrc[n], ircv[n], ilive[n], l_ref, r_ref)

    ready(0, l0, r0)
    ready(1, l1, r1)
    multiply(l0, r0, q0, 3 * LANES)
    multiply(l1, r1, q1, 3 * LANES)
    ready(2, l0, r0)
    ready(3, l1, r1)

    def step(p, state):
        e0, e1, o0, o1 = state
        i = 2 * p
        prev = jnp.where(p == 0, count, i - 2)
        finish(prev, [e0, e1])
        finish(prev + 1, [o0, o1])
        e0, e1 = kernel_sum(i, q0, [o0, o1])
        multiply(l0, r0, q0, 3 * LANES)
        ready(i + 4, l0, r0)
        o0, o1 = kernel_sum(i + 1, q1, [e0, e1])
        multiply(l1, r1, q1, 3 * LANES)
        ready(i + 5, l1, r1)
        return e0, e1, o0, o1

    steps = lax.shift_right_logical(count + 1, 1)
    e0, e1, o0, o1 = lax.fori_loop(0, steps, step, (zero, zero, zero, zero))
    finish(2 * steps - 2, [e0, e1])
    finish(2 * steps - 1, [o0, o1])

    def fready(n, l_ref, r_ref, m_ref):
        src, slot, live = fsrc[n], 2 * fslot[n], flive[n]
        rcv = home + 2 * jnp.where(fcell[n] == 1, 1, 0)
        for c, d in enumerate(prepare(src, rcv, live, l_ref, r_ref)):
            m = spread(d, 3) * live
            rho = jnp.broadcast_to(rrow[pl.ds(slot + c, 1), :], (8, LANES))
            w = jnp.where(m > 0.0, m / rho, 0.0)
            one = jnp.where(space, d, jnp.where(sub == 3, 1.0, 0.0))
            a = split3(one * m)
            b = split3(one * w)
            m_ref[:, c * LANES : (c + 1) * LANES] = jnp.concatenate(
                [stack16(a[k], b[k]) for k in range(3)], 0
            )

    def force_sum(n, q_ref, m_ref, before):
        keep = fkeep[n]
        sums = None
        for c in range(2):
            high, low = [], []
            for g in range(LANES // 16):
                cut = slice(c * LANES + 16 * g, c * LANES + 16 * g + 16)
                t = nearness(q_ref[cut, 0 : 2 * LANES])
                t3 = t * t * t
                hi = t3.astype(jnp.bfloat16)
                high.append(hi)
                low.append((t3 - hi.astype(jnp.float32)).astype(jnp.bfloat16))
            left = m_ref[:, c * LANES : (c + 1) * LANES]
            for part in (high, low):
                out = jnp.dot(left, jnp.concatenate(part, 0), preferred_element_type=jnp.float32)
                sums = out if sums is None else sums + out
        both = sums[0:16] + sums[16:32] + sums[32:48]
        return [
            before[2 * k + c] * keep + both[8 * k : 8 * k + 8, c * LANES : (c + 1) * LANES]
            for k in range(2)
            for c in range(2)
        ]

    def settle(n, acc):
        j = fcell[n]
        own = jnp.where(j == 1, 1, 0)
        rcv = home + 2 * own
        mid = centre(rcv)
        for c in range(2):
            v = rows8(rcv + c)
            d = v - mid
            rho = jnp.broadcast_to(rrow[pl.ds(2 * (32 + 2 * member + own) + c, 1), :], (8, LANES))
            both = acc[c] * jnp.where(spread(v, 3) > 0.0, 1.0 / rho, 0.0) + acc[2 + c]
            h = spread(v, 4)
            h2 = h * h
            scale = jnp.where(spread(v, 3) > 0.0, NORM_F / (h2 * h2 * h), 0.0)
            orow[pl.ds(pl.multiple_of(j * 16 + c * 8, 8), 8), :] = (d * spread(both, 3) - both) * scale

    fready(0, l0, r0, m0)
    fready(1, l1, r1, m1)
    multiply(l0, r0, q0, 2 * LANES)
    multiply(l1, r1, q1, 2 * LANES)

    def fpair(p, state):
        i = 2 * p
        prev = jnp.where(p == 0, total, i - 2)
        settle(prev, state[0:4])
        settle(prev + 1, state[4:8])
        even = force_sum(i, q0, m0, state[4:8])
        fready(i + 2, l0, r0, m0)
        multiply(l0, r0, q0, 2 * LANES)
        odd = force_sum(i + 1, q1, m1, even)
        fready(i + 3, l1, r1, m1)
        multiply(l1, r1, q1, 2 * LANES)
        return (*even, *odd)

    steps = lax.shift_right_logical(total + 1, 1)
    state = lax.fori_loop(0, steps, fpair, (zero,) * 8)
    settle(jnp.where(steps == 0, total, 2 * steps - 2), state[0:4])
    settle(jnp.where(steps == 0, total, 2 * steps - 1), state[4:8])

    for j in range(2):
        for c in range(2):
            cut = pl.ds((2 * j + c) * LANES, LANES)
            rho = rrow[pl.ds(2 * (32 + 2 * member + j) + c, 1), :]
            dens_ref[cut] = jnp.where(row(home + 2 * j + c, 3) > 0.0, rho, 0.0).reshape(LANES)
            r = j * 16 + c * 8
            acc_ref[:, cut] = orow[r : r + 3, :]


def main_call(pool, member_of, interpret=False):
    def ints(n):
        return pltpu.SMEM((n,), jnp.int32)

    def floats(n):
        return pltpu.SMEM((n,), jnp.float32)

    def pair(*shape):
        return [pltpu.VMEM(shape[:2], shape[2])] * 2

    return pl.pallas_call(
        lambda *refs: main_kernel(member_of, *refs),
        out_shape=(jax.ShapeDtypeStruct((512,), jnp.float32), jax.ShapeDtypeStruct((3, 512), jnp.float32)),
        in_specs=[pl.BlockSpec(memory_space=pltpu.VMEM)],
        out_specs=(pl.BlockSpec(memory_space=pltpu.VMEM), pl.BlockSpec(memory_space=pltpu.VMEM)),
        scratch_shapes=[
            pltpu.VMEM((16, LANES), jnp.int32),
            pltpu.SMEM((16, LANES), jnp.int32),
            pltpu.SemaphoreType.DMA,
            ints(96),
            ints(192),
            ints(192),
            ints(192),
            floats(192),
            floats(192),
            ints(24),
            ints(24),
            ints(24),
            floats(24),
            floats(24),
            *pair(CELL, LANES, jnp.bfloat16),
            *pair(48, 3 * LANES, jnp.bfloat16),
            *pair(48, CELL, jnp.bfloat16),
            *pair(CELL, 3 * LANES, jnp.float32),
            pltpu.VMEM((200, LANES), jnp.float32),
            pltpu.VMEM((48, LANES), jnp.float32),
        ],
        interpret=interpret,
        name="sph",
    )(pool)


def pack_call(positions, mass, smooth, counts, tasks, member_of, interpret=False):
    smem = pl.BlockSpec(memory_space=pltpu.SMEM)
    vmem = pl.BlockSpec(memory_space=pltpu.VMEM)
    return pl.pallas_call(
        lambda *refs: pack_kernel(member_of, *refs),
        out_shape=jax.ShapeDtypeStruct((ROWS, LANES), jnp.float32),
        in_specs=[smem, smem, vmem, vmem, vmem],
        out_specs=vmem,
        interpret=interpret,
        name="pack",
    )(counts, tasks, positions, mass, smooth)


def shifted(block, step):
    count = lax.axis_size("dom")
    return lax.ppermute(block, "dom", [(i, (i + step) % count) for i in range(count)])


def local(positions, mass, smooth, counts, tasks):
    block = pack_call(positions, mass, smooth, counts, tasks, lambda: lax.axis_index("grp"))
    low, high = shifted(block, 1), shifted(block, -1)
    low2, high2 = shifted(block, 2), shifted(block, -2)
    wide = jnp.concatenate([low2[:FAR], high2[:FAR], low, block, high], 0)
    pool = lax.all_gather(wide, "grp", axis=0, tiled=True)
    return main_call(pool, lambda: lax.axis_index("grp"))


def solution(mesh):
    in_specs = (
        P(None, ("dom", "grp")),
        P(("dom", "grp")),
        P(("dom", "grp")),
        P(("dom", "grp")),
        P(None, ("dom", "grp")),
    )
    out_specs = (P(("dom", "grp")), P(None, ("dom", "grp")))
    return jax.shard_map(local, mesh=mesh, in_specs=in_specs, out_specs=out_specs, check_vma=False)
```

```python
import math

import jax
import jax.numpy as jnp
from jax import lax
from jax.experimental import pallas as pl
from jax.experimental.pallas import tpu as pltpu
from jax.sharding import PartitionSpec as P

CELL = 256
LANES = 128
ROWS = 24
FAR = 16
BLOCK = 3 * ROWS + 2 * FAR
NORM_W = 21.0 / (2.0 * math.pi)
NORM_F = 105.0 / math.pi
TINY = 1e-30


def pack_kernel(member_of, counts_ref, tasks_ref, pos_ref, mass_ref, smooth_ref, out_ref, tmp):
    lane = lax.broadcasted_iota(jnp.int32, (1, LANES), 1)
    for j in range(2):
        for c in range(2):
            row = 2 * j + c
            cut = pl.ds(row * LANES, LANES)
            for axis in range(3):
                tmp[4 * axis + row : 4 * axis + row + 1, :] = pos_ref[axis : axis + 1, cut]
            live = lane + c * LANES < counts_ref[j]
            tmp[12 + row : 13 + row, :] = jnp.where(live, mass_ref[cut].reshape(1, LANES), 0.0)
            tmp[16 + row : 17 + row, :] = smooth_ref[cut].reshape(1, LANES)
    codes = jnp.zeros((1, LANES), jnp.float32)
    place = lane - 4 * member_of()
    for i in range(4):
        codes = jnp.where(place == i, tasks_ref[0, i].astype(jnp.float32), codes)
        codes = jnp.where(place == 64 + i, tasks_ref[1, i].astype(jnp.float32), codes)
    tmp[20:21, :] = codes
    tmp[21:24, :] = jnp.zeros((3, LANES), jnp.float32)
    for k in range(4):
        out_ref[k] = tmp[...]


def place_of(member):
    return (member & 1) * 8 + lax.shift_right_logical(member, 1)


def split3(v):
    a = v.astype(jnp.bfloat16).astype(jnp.float32)
    b = (v - a).astype(jnp.bfloat16).astype(jnp.float32)
    return a, b, v - a - b


def stack16(*parts):
    return jnp.concatenate(parts, 0).astype(jnp.bfloat16)


def main_kernel(
    member_of, g_ref, dens_ref, acc_ref, tvm, tsm, sem, done, isrc, ircv, islot, ikeep, ilive,
    fsrc, fslot, fcell, fkeep, flive, l0, l1, r0, r1, m0, m1, q0, q1, rrow, orow,
):
    wide = (64, LANES)
    lane = lax.broadcasted_iota(jnp.int32, wide, 1)
    other = lax.broadcasted_iota(jnp.int32, wide, 0)
    codes = []
    for s in range(3):
        at = 2 * FAR + s * ROWS + 20
        both = jnp.concatenate([g_ref[m * BLOCK + at : m * BLOCK + at + 1, :] for m in range(16)], 0)
        codes.append(jnp.sum(both, 0, keepdims=True))
    turned = jnp.transpose(jnp.concatenate(codes + [jnp.zeros((5, LANES), jnp.float32)], 0))
    lane1 = lax.broadcasted_iota(jnp.int32, (1, LANES), 1)
    lists = []
    for s in range(3):
        mine = jnp.broadcast_to(turned[0:64, s : s + 1], wide).astype(jnp.int32)
        code = codes[s].astype(jnp.int32)
        theirs = jnp.broadcast_to(code, wide)
        later = jnp.max(jnp.where((mine == theirs) & (other < lane), other, -1), 0, keepdims=True)
        head = jnp.max(jnp.where(mine == lane - 64, other, -1), 0, keepdims=True)
        slab = lax.shift_right_logical(code, 5) + s
        cell = code & 31
        base = jnp.where(slab == 0, 0, jnp.where(slab == 4, FAR, slab * ROWS + (2 * FAR - ROWS)))
        where = place_of(lax.shift_right_logical(cell, 1)) * BLOCK + base + 2 * (cell & 1)
        lists.append(jnp.where(lane1 < 64, later, where))
        lists.append(jnp.where(lane1 < 64, (slab - 1) * 32 + cell, head))
        lists.append((slab - 1) * 32 + cell)
    tvm[...] = jnp.concatenate(lists + [jnp.zeros((7, LANES), jnp.int32)], 0)
    copy = pltpu.make_async_copy(tvm, tsm, sem)
    copy.start()

    def clear(i, _):
        for k in range(16):
            done[16 * i + k] = 0
        return 0

    lax.fori_loop(0, 6, clear, 0)
    orow[...] = jnp.zeros((48, LANES), jnp.float32)
    member = member_of()
    home = place_of(member) * BLOCK + 2 * FAR + ROWS
    copy.wait()

    def list_cell(cell, n):
        s = lax.shift_right_logical(cell, 5)
        c = cell & 31
        rcv = place_of(lax.shift_right_logical(c, 1)) * BLOCK + s * ROWS + 2 * FAR + 2 * (c & 1)
        slot = 2 * cell
        ahead = 3 * s

        def put(n, src, keep, live):
            isrc[n] = src
            ircv[n] = rcv
            islot[n] = slot
            ikeep[n] = keep
            ilive[n] = live

        def add(state):
            t, n = state
            put(n, tsm[ahead, 64 + t], 1.0, 1.0)
            return tsm[ahead, t], n + 1

        put(n, rcv, 0.0, 0.0)
        _, last = lax.while_loop(lambda s: s[0] >= 0, add, (tsm[ahead + 1, 64 + c], n))
        ikeep[n] = 0.0
        done[cell] = 1
        return jnp.maximum(last, n + 1)

    count = jnp.int32(0)
    total = jnp.int32(0)
    for j in range(2):
        cell = 32 + 2 * member + j
        count = list_cell(cell, count)
        start = total

        def own(state, j=j):
            t, n = state
            fsrc[n] = tsm[3, 64 + t]
            fslot[n] = tsm[5, 64 + t]
            fcell[n] = j
            fkeep[n] = 1.0
            flive[n] = 1.0
            return tsm[3, t], n + 1

        _, total = lax.while_loop(lambda s: s[0] >= 0, own, (tsm[4, 64 + 2 * member + j], total))
        fkeep[start] = 0.0

    def need(i, n):
        cell = fslot[i]
        return lax.cond(done[cell] == 0, lambda n: list_cell(cell, n), lambda n: n, n)

    count = lax.fori_loop(0, total, need, count)
    for k in range(6):
        isrc[count + k] = home
        ircv[count + k] = home
        islot[count + k] = 192
        ikeep[count + k] = 0.0
        ilive[count + k] = 0.0
        fsrc[total + k] = home
        fslot[total + k] = 32 + 2 * member
        fcell[total + k] = 2
        fkeep[total + k] = 0.0
        flive[total + k] = 0.0

    sub = lax.broadcasted_iota(jnp.int32, (8, LANES), 0)
    space = sub < 3
    pad = jnp.zeros((2, LANES), jnp.float32)

    def rows8(row):
        return jnp.concatenate([g_ref[pl.ds(row, 6, stride=4), :], pad], 0)

    def spread(v, k):
        return jnp.broadcast_to(v[k : k + 1, :], (8, LANES))

    def centre(rcv):
        return jnp.where(space, jnp.broadcast_to(rows8(rcv)[:, 0:1], (8, LANES)), 0.0)

    def square(d):
        return jnp.broadcast_to(jnp.sum(jnp.where(space, d * d, 0.0), 0, keepdims=True), (8, LANES))

    lanes8 = lax.broadcasted_iota(jnp.int32, (48, LANES), 0)
    pick_mass = jnp.where((lanes8 == 5) | (lanes8 == 13) | (lanes8 == 37), 1.0, 0.0).astype(jnp.bfloat16)
    for r_ref in (r0, r1):
        r_ref[:, 2 * LANES : 3 * LANES] = pick_mass

    def prepare(src, rcv, live, l_ref, r_ref):
        mid = centre(rcv)
        out = []
        for c in range(2):
            d = rows8(src + c) - mid
            out.append(d)
            b = jnp.where(space, d, jnp.where(sub == 3, 1.0, jnp.where(sub == 4, square(d), 0.0)))
            b = jnp.where(sub == 5, spread(d, 3) * live, b)
            b1, b2, b3 = split3(b)
            pair = stack16(b1, b2)
            left = jnp.concatenate([pair, pair, stack16(b3, b1)], 0)
            l_ref[c * LANES : (c + 1) * LANES, 0:48] = jnp.transpose(left)
            v = rows8(rcv + c)
            d = v - mid
            h = spread(v, 4)
            s = 1.0 / (h * h)
            a = jnp.where(space, -2.0 * d, jnp.where(sub == 3, square(d), jnp.where(sub == 4, 1.0, 0.0))) * s
            a1, a2, a3 = split3(a)
            r_ref[:, c * LANES : (c + 1) * LANES] = jnp.concatenate(
                [stack16(a1, a1), stack16(a2, a2), stack16(a1, a3)], 0
            )
        return out

    def multiply(l_ref, r_ref, q_ref, width):
        q_ref[:, 0:width] = jnp.dot(
            l_ref[:, 0:48], r_ref[:, 0:width], preferred_element_type=jnp.float32
        )

    def nearness(q2):
        q2 = jnp.maximum(q2, TINY)
        return jnp.maximum(1.0 - q2 * lax.rsqrt(q2), 0.0)

    def kernel_sum(n, q_ref, before):
        keep = ikeep[n]
        acc = [v * keep for v in before]
        for g in range(CELL // 8):
            cut = slice(8 * g, 8 * g + 8)
            m = q_ref[cut, 2 * LANES : 3 * LANES]
            for c in range(2):
                t = nearness(q_ref[cut, c * LANES : (c + 1) * LANES])
                t2 = t * t
                acc[c] = acc[c] + (t2 * t2) * (1.25 - t) * m
        return acc

    def row(r, q):
        return g_ref[pl.ds(r + 4 * q, 1), :]

    def finish(n, acc):
        rcv, slot = ircv[n], islot[n]
        for c in range(2):
            h = row(rcv + c, 4)
            total = 4.0 * jnp.sum(acc[c], 0, keepdims=True) + row(rcv + c, 3)
            rrow[pl.ds(slot + c, 1), :] = total * (NORM_W / (h * h * h))

    zero = jnp.zeros((8, LANES), jnp.float32)

    def ready(n, l_ref, r_ref):
        prepare(isrc[n], ircv[n], ilive[n], l_ref, r_ref)

    ready(0, l0, r0)
    ready(1, l1, r1)
    multiply(l0, r0, q0, 3 * LANES)
    multiply(l1, r1, q1, 3 * LANES)
    ready(2, l0, r0)
    ready(3, l1, r1)

    def step(p, state):
        e0, e1, o0, o1 = state
        i = 2 * p
        prev = jnp.where(p == 0, count, i - 2)
        finish(prev, [e0, e1])
        finish(prev + 1, [o0, o1])
        e0, e1 = kernel_sum(i, q0, [o0, o1])
        multiply(l0, r0, q0, 3 * LANES)
        ready(i + 4, l0, r0)
        o0, o1 = kernel_sum(i + 1, q1, [e0, e1])
        multiply(l1, r1, q1, 3 * LANES)
        ready(i + 5, l1, r1)
        return e0, e1, o0, o1

    steps = lax.shift_right_logical(count + 1, 1)
    e0, e1, o0, o1 = lax.fori_loop(0, steps, step, (zero, zero, zero, zero))
    finish(2 * steps - 2, [e0, e1])
    finish(2 * steps - 1, [o0, o1])

    def fready(n, l_ref, r_ref, m_ref):
        src, slot, live = fsrc[n], 2 * fslot[n], flive[n]
        rcv = home + 2 * jnp.where(fcell[n] == 1, 1, 0)
        for c, d in enumerate(prepare(src, rcv, live, l_ref, r_ref)):
            m = spread(d, 3) * live
            rho = jnp.broadcast_to(rrow[pl.ds(slot + c, 1), :], (8, LANES))
            w = jnp.where(m > 0.0, m / rho, 0.0)
            one = jnp.where(space, d, jnp.where(sub == 3, 1.0, 0.0))
            a = split3(one * m)
            b = split3(one * w)
            m_ref[:, c * LANES : (c + 1) * LANES] = jnp.concatenate(
                [stack16(a[k], b[k]) for k in range(3)], 0
            )

    def force_sum(n, q_ref, m_ref, before):
        keep = fkeep[n]
        sums = None
        for c in range(2):
            high, low = [], []
            for g in range(LANES // 16):
                cut = slice(c * LANES + 16 * g, c * LANES + 16 * g + 16)
                t = nearness(q_ref[cut, 0 : 2 * LANES])
                t3 = t * t * t
                hi = t3.astype(jnp.bfloat16)
                high.append(hi)
                low.append((t3 - hi.astype(jnp.float32)).astype(jnp.bfloat16))
            left = m_ref[:, c * LANES : (c + 1) * LANES]
            for part in (high, low):
                out = jnp.dot(left, jnp.concatenate(part, 0), preferred_element_type=jnp.float32)
                sums = out if sums is None else sums + out
        both = sums[0:16] + sums[16:32] + sums[32:48]
        return [
            before[2 * k + c] * keep + both[8 * k : 8 * k + 8, c * LANES : (c + 1) * LANES]
            for k in range(2)
            for c in range(2)
        ]

    def settle(n, acc):
        j = fcell[n]
        own = jnp.where(j == 1, 1, 0)
        rcv = home + 2 * own
        mid = centre(rcv)
        for c in range(2):
            v = rows8(rcv + c)
            d = v - mid
            rho = jnp.broadcast_to(rrow[pl.ds(2 * (32 + 2 * member + own) + c, 1), :], (8, LANES))
            both = acc[c] * jnp.where(spread(v, 3) > 0.0, 1.0 / rho, 0.0) + acc[2 + c]
            h = spread(v, 4)
            h2 = h * h
            scale = jnp.where(spread(v, 3) > 0.0, NORM_F / (h2 * h2 * h), 0.0)
            orow[pl.ds(pl.multiple_of(j * 16 + c * 8, 8), 8), :] = (d * spread(both, 3) - both) * scale

    fready(0, l0, r0, m0)
    fready(1, l1, r1, m1)
    multiply(l0, r0, q0, 2 * LANES)
    multiply(l1, r1, q1, 2 * LANES)

    def fpair(p, state):
        i = 2 * p
        prev = jnp.where(p == 0, total, i - 2)
        settle(prev, state[0:4])
        settle(prev + 1, state[4:8])
        even = force_sum(i, q0, m0, state[4:8])
        fready(i + 2, l0, r0, m0)
        multiply(l0, r0, q0, 2 * LANES)
        odd = force_sum(i + 1, q1, m1, even)
        fready(i + 3, l1, r1, m1)
        multiply(l1, r1, q1, 2 * LANES)
        return (*even, *odd)

    steps = lax.shift_right_logical(total + 1, 1)
    state = lax.fori_loop(0, steps, fpair, (zero,) * 8)
    settle(jnp.where(steps == 0, total, 2 * steps - 2), state[0:4])
    settle(jnp.where(steps == 0, total, 2 * steps - 1), state[4:8])

    for j in range(2):
        for c in range(2):
            cut = pl.ds((2 * j + c) * LANES, LANES)
            rho = rrow[pl.ds(2 * (32 + 2 * member + j) + c, 1), :]
            dens_ref[cut] = jnp.where(row(home + 2 * j + c, 3) > 0.0, rho, 0.0).reshape(LANES)
            r = j * 16 + c * 8
            acc_ref[:, cut] = orow[r : r + 3, :]


def main_call(pool, member_of, interpret=False):
    def ints(n):
        return pltpu.SMEM((n,), jnp.int32)

    def floats(n):
        return pltpu.SMEM((n,), jnp.float32)

    def pair(*shape):
        return [pltpu.VMEM(shape[:2], shape[2])] * 2

    return pl.pallas_call(
        lambda *refs: main_kernel(member_of, *refs),
        out_shape=(jax.ShapeDtypeStruct((512,), jnp.float32), jax.ShapeDtypeStruct((3, 512), jnp.float32)),
        in_specs=[pl.BlockSpec(memory_space=pltpu.VMEM)],
        out_specs=(pl.BlockSpec(memory_space=pltpu.VMEM), pl.BlockSpec(memory_space=pltpu.VMEM)),
        scratch_shapes=[
            pltpu.VMEM((16, LANES), jnp.int32),
            pltpu.SMEM((16, LANES), jnp.int32),
            pltpu.SemaphoreType.DMA,
            ints(96),
            ints(192),
            ints(192),
            ints(192),
            floats(192),
            floats(192),
            ints(24),
            ints(24),
            ints(24),
            floats(24),
            floats(24),
            *pair(CELL, LANES, jnp.bfloat16),
            *pair(48, 3 * LANES, jnp.bfloat16),
            *pair(48, CELL, jnp.bfloat16),
            *pair(CELL, 3 * LANES, jnp.float32),
            pltpu.VMEM((200, LANES), jnp.float32),
            pltpu.VMEM((48, LANES), jnp.float32),
        ],
        interpret=interpret,
        name="sph",
    )(pltpu.with_memory_space_constraint(pool, pltpu.VMEM))


def pack_call(positions, mass, smooth, counts, tasks, member_of, interpret=False):
    smem = pl.BlockSpec(memory_space=pltpu.SMEM)
    vmem = pl.BlockSpec(memory_space=pltpu.VMEM)
    return pl.pallas_call(
        lambda *refs: pack_kernel(member_of, *refs),
        out_shape=jax.ShapeDtypeStruct((4, ROWS, LANES), jnp.float32),
        in_specs=[smem, smem, vmem, vmem, vmem],
        out_specs=vmem,
        scratch_shapes=[pltpu.VMEM((ROWS, LANES), jnp.float32)],
        interpret=interpret,
        name="pack",
    )(counts, tasks, positions, mass, smooth)


def along_x(copies):
    rows = [[4 * y + x for x in range(4)] for y in range(lax.axis_size("dom") // 4)]
    return lax.all_to_all(copies, "dom", 0, 0, axis_index_groups=rows)


def pick(x, options):
    out = options[3]
    for k in range(3):
        out = jnp.where(x == k, options[k], out)
    return out


def halo(copies):
    count = lax.axis_size("dom")
    x = lax.axis_index("dom") % 4
    r = along_x(copies)
    ends = jnp.where(x < 2, r[2:4], r[0:2])
    step = [(i, (i + (4 if i % 4 < 2 else -4)) % count) for i in range(count)]
    w = lax.ppermute(ends, "dom", step)
    return (
        pick(x, (w[0], w[1], r[0], r[1])),
        pick(x, (r[2], r[3], w[0], w[1])),
        pick(x, (w[1], r[0], r[1], r[2])),
        pick(x, (r[0], r[1], r[2], r[3])),
        pick(x, (r[1], r[2], r[3], w[0])),
    )


def gather(wide):
    members = lax.axis_size("grp")
    stacks = [list(range(c, members, 2)) for c in range(2)]
    pairs = [[m, m + 1] for m in range(0, members, 2)]
    copies = jnp.broadcast_to(wide[None], (members // 2, BLOCK, LANES))
    half = lax.all_to_all(copies, "grp", 0, 0, axis_index_groups=stacks)
    return lax.all_gather(half, "grp", axis_index_groups=pairs).reshape(members * BLOCK, LANES)


def local(positions, mass, smooth, counts, tasks):
    copies = pack_call(positions, mass, smooth, counts, tasks, lambda: lax.axis_index("grp"))
    low2, high2, low, own, high = halo(copies)
    pool = gather(jnp.concatenate([low2[:FAR], high2[:FAR], low, own, high], 0))
    return main_call(pool, lambda: lax.axis_index("grp"))


def solution(mesh):
    in_specs = (
        P(None, ("dom", "grp")),
        P(("dom", "grp")),
        P(("dom", "grp")),
        P(("dom", "grp")),
        P(None, ("dom", "grp")),
    )
    out_specs = (P(("dom", "grp")), P(None, ("dom", "grp")))
    return jax.shard_map(local, mesh=mesh, in_specs=in_specs, out_specs=out_specs, check_vma=False)
```
